32 devices in a mesh: dp: 16 (over z, y, x), tensor: 2 (over core).
Axes of the slice: x: 2, y: 2, z: 4, core: 2. Of those that a mesh axis runs over, the one named last changes fastest.
Arguments:
- tokens: bfloat16 [32768, 1024], P(('dp', 'tensor')), may hold values from -6 to 6
- cotangent: bfloat16 [32768, 1024], P(('dp', 'tensor')), may hold values from -6 to 6
- qkv_w: float32 [1024, 3, 1024], P('dp', None, 'tensor'), may hold values from -0.1875 to 0.1875
- out_w: float32 [1024, 1024], P('tensor', 'dp'), may hold values from -4 to 4
- ffin_w: float32 [1024, 2, 2624], P('dp', None, 'tensor'), may hold values from -0.1875 to 0.1875
- ffout_w: float32 [2624, 1024], P('tensor', 'dp'), may hold values from -0.125 to 0.125
- norm1: float32 [1024], P('dp'), may hold values from 0.5 to 1.5
- norm2: float32 [1024], P('dp'), may hold values from 0.5 to 1.5
- lengths: int32 [16], replicated, may hold values from 1024 to 2048, as said below
- assign: int32 [16], replicated, may hold values from 0 to 15, each once
Outputs:
- mixed: bfloat16 [32768, 1024], P(('dp', 'tensor'))
- grad_tokens: float32 [32768, 1024], P(('dp', 'tensor'))
- grad_qkv: float32 [1024, 3, 1024], P('dp', None, 'tensor')
- grad_out: float32 [1024, 1024], P('tensor', 'dp')
- grad_ffin: float32 [1024, 2, 2624], P('dp', None, 'tensor')
- grad_ffout: float32 [2624, 1024], P('tensor', 'dp')
- grad_norm1: float32 [1024], P('dp')
- grad_norm2: float32 [1024], P('dp')
The draws below stay inside these ranges and needn't reach their ends.
Inputs may be any that keep to these rules, and one draw needn't show every extreme that they name: lengths[i] valid tokens fill the first slots of sequence i; one sequence has exactly 2048, another exactly 1024. Data group g holds sequence assign[g]; every sequence once.
All inputs are finite; a program needn't handle non-finite values.
Results may differ from the reference program's by a relative error of at most 0.023.
Values may be sent and summed in bfloat16 or wider, within the bound.
No kernel may reach another device: no remote copies, remote signals or barrier semaphores. Data moves between devices by JAX's collectives and lax.ppermute only.
A program may use at most 256 MiB of HBM per device.

```python
import jax
import jax.numpy as jnp
from jax import lax

D = 1024
HEADS = 16
HEAD_DIM = 64
FF = 2624
SLOTS = 2048
LEAST = 1024
SEQS = 16
TOKENS = 32768
N_DP = 16


def draw_lengths(key, part):
    first = jax.random.randint(jax.random.fold_in(key, 11), (SEQS,), 0, SLOTS - LEAST + 1)
    second = jax.random.randint(jax.random.fold_in(key, 12), (SEQS,), 0, SLOTS - LEAST + 1)
    longest = jax.random.randint(jax.random.fold_in(key, 13), (), 0, SEQS)
    offset = jax.random.randint(jax.random.fold_in(key, 14), (), 1, SEQS)
    shortest = (longest + offset) % SEQS
    length_all = LEAST + jnp.minimum(first, second)
    places = jnp.arange(SEQS)
    length_all = jnp.where(places == longest, SLOTS, length_all)
    length_all = jnp.where(places == shortest, LEAST, length_all)
    return length_all.astype(jnp.int32)


def strengthened(array, own_key, source, target, blocks, factor):
    owner, partner = [(jnp.arange(array.shape[position]) // (array.shape[position] // blocks)).reshape([-1 if axis == position else 1 for axis in range(array.ndim)]) for position in (source, target)]
    chosen = jax.random.permutation(own_key, blocks)[partner]
    strong = (owner == chosen) | (owner == (partner + blocks // 2) % blocks)
    return jnp.where(strong, factor * array, array)


def block_scale(key, dims, split, least, high):
    loudness = 1.0
    for axis_at, blocks in split:
        steps = jax.random.uniform(jax.random.fold_in(jax.random.fold_in(key, 6), axis_at), (blocks,), jnp.float32, least / len(split), high / len(split))
        loudness = loudness * jnp.repeat(jnp.exp(steps), dims[axis_at] // blocks).reshape((-1,) + (1,) * (len(dims) - 1 - axis_at))
    return loudness


def bell_draw(stream_key, dims, width, bound, shards=(), dtype=jnp.bfloat16):
    entries = width * jax.random.normal(stream_key, dims, jnp.float32)
    if shards:
        entries = entries * block_scale(stream_key, dims, shards, -0.22, 0.18)
    return jnp.clip(entries, -bound, bound).astype(dtype)


def bell_draw_with(key, dims, scale, bound, split, heavy, held_as=jnp.bfloat16):
    values = scale * jax.random.normal(key, dims, jnp.float32)
    if split:
        values = values * block_scale(key, dims, split, -0.22, 0.18)
    return jnp.clip(strengthened(values, jax.random.fold_in(key, 3), *heavy), -bound, bound).astype(held_as)


def setup_inputs(seed: int = 0) -> dict:
    seeds = jax.random.split(jax.random.key(seed), 11)
    return {
        "tokens": bell_draw_with(seeds[0], (TOKENS, D), 1.0, 6.0, ((0, 32),), (0, 1, 32, 2.75)),
        "cotangent": bell_draw_with(seeds[1], (TOKENS, D), 1.0, 6.0, ((0, 32),), (0, 1, 32, 2.75)),
        "qkv_w": bell_draw(seeds[2], (D, 3, D), D ** -0.5, 0.1875, ((0, 16), (2, 2)), jnp.float32),
        "out_w": bell_draw(seeds[3], (D, D), 2 ** -0.5, 4.0, ((0, 2), (1, 16)), jnp.float32),
        "ffin_w": bell_draw(seeds[4], (D, 2, FF), D ** -0.5, 0.1875, ((0, 16), (2, 2)), jnp.float32),
        "ffout_w": bell_draw(seeds[5], (FF, D), FF ** -0.5, 0.125, ((0, 2), (1, 16)), jnp.float32),
        "norm1": jnp.clip(1.0 + 0.1 * jax.random.normal(seeds[6], (D,), jnp.float32), 0.5, 1.5),
        "norm2": jnp.clip(1.0 + 0.1 * jax.random.normal(seeds[7], (D,), jnp.float32), 0.5, 1.5),
        "lengths": draw_lengths(jax.random.fold_in(seeds[10], 71), 0),
        "assign": jax.random.permutation(seeds[9], SEQS).astype(jnp.int32),
    }


@jax.custom_vjp
def low(v):
    return lax.optimization_barrier(v.astype(jnp.bfloat16)).astype(jnp.float32)

@jax.custom_vjp
def low_back(v):
    return v

def low_keep(v):
    return (low(v), None)

def low_pass(kept, grad):
    return (grad,)

def back_keep(v):
    return (v, None)

def back_low(kept, grad):
    return (low(grad),)
low.defvjp(low_keep, low_pass)
low_back.defvjp(back_keep, back_low)
epsilon = 1e-05
rope_base = 160000.0

def precise_dot(left, right):
    return jnp.dot(left, right, precision=lax.Precision.HIGHEST)

def layer_norm(stream, gain_vec):
    center = stream - lax.optimization_barrier(jnp.mean(stream, axis=-1, keepdims=True))
    spread = lax.optimization_barrier(jnp.mean(center * center, axis=-1, keepdims=True))
    return center * lax.rsqrt(spread + epsilon) * gain_vec

def rope_tables(length_all):
    index = jnp.arange(HEAD_DIM // 2).astype(jnp.float32)
    inverse = rope_base ** (-2.0 * index / HEAD_DIM)
    places = jnp.arange(length_all).astype(jnp.float32)
    angle = places[:, None] * inverse[None, :]
    angle = jnp.concatenate([angle, angle], axis=1)
    return (jnp.cos(angle), jnp.sin(angle))

def rotary(vectors, cosine, sine):
    middle = vectors.shape[-1] // 2
    turned = jnp.concatenate([-vectors[..., middle:], vectors[..., :middle]], axis=-1)
    return vectors * cosine[:, None, :] + turned * sine[:, None, :]

def attention(queries, keys_all, values_all, key_live):
    slots = queries.shape[0]
    block_rows = min(512, slots)
    query_blocks = queries.reshape(slots // block_rows, block_rows, HEADS, HEAD_DIM)
    scale = HEAD_DIM ** (-0.5)

    def one_block(query_block):
        scores = jnp.einsum('qhd,khd->hqk', query_block, keys_all, precision=lax.Precision.HIGHEST) * scale
        scores = low_back(scores)
        scores = jnp.where(key_live[None, None, :], scores, -1e+30)
        row_max = lax.optimization_barrier(jnp.max(scores, axis=-1, keepdims=True))
        log_total = row_max + jnp.log(lax.optimization_barrier(jnp.sum(jnp.exp(scores - row_max), axis=-1, keepdims=True)))
        prob_rows = jnp.exp(scores - log_total)
        return jnp.einsum('hqk,khd->qhd', low(prob_rows), values_all, precision=lax.Precision.HIGHEST)
    result = lax.map(jax.checkpoint(one_block), query_blocks)
    return result.reshape(slots, HEADS, HEAD_DIM)

def forward(stream, qkv_w, out_w, ffin_w, ffout_w, norm1, norm2, length):
    slots = stream.shape[0]
    gain_one = low(norm1)
    gain_two = low(norm2)
    w_qkv = low(qkv_w).reshape(D, 3 * D)
    w_out = low(out_w)
    w_in = low(ffin_w).reshape(D, 2 * FF)
    w_down = low(ffout_w)
    key_live = jnp.arange(slots) < length
    normed_one = low(layer_norm(stream, gain_one))
    project = low_back(precise_dot(normed_one, w_qkv)).reshape(slots, 3, HEADS, HEAD_DIM)
    cosine, sine = rope_tables(slots)
    queries = low(rotary(project[:, 0], cosine, sine))
    keys_all = low(rotary(project[:, 1], cosine, sine))
    values_all = low(project[:, 2])
    attended = attention(queries, keys_all, values_all, key_live)
    attended = low(low_back(attended)).reshape(slots, D)
    branch = low_back(precise_dot(attended, w_out))
    middle = stream + branch
    normed_two = low(layer_norm(middle, gain_two))
    gate_up = precise_dot(normed_two, w_in).reshape(slots, 2, FF)
    gate_part = low_back(gate_up[:, 0])
    up_part = low_back(gate_up[:, 1])
    hidden = low(jax.nn.gelu(gate_part, approximate=False) * up_part)
    feed = low_back(precise_dot(hidden, w_down))
    return jnp.where(key_live[:, None], middle + feed, 0.0)

def reference(tokens, cotangent, qkv_w, out_w, ffin_w, ffout_w, norm1, norm2, lengths, assign):
    streams = tokens.astype(jnp.float32).reshape(N_DP, SLOTS, D)
    grads_in = cotangent.astype(jnp.float32).reshape(N_DP, SLOTS, D)
    owned = jnp.take(lengths, assign).astype(jnp.int32)
    weights = (qkv_w, out_w, ffin_w, ffout_w, norm1, norm2)
    totals = jax.tree.map(jnp.zeros_like, weights)

    def one_sequence(carry, item):
        stream, grad_seq, length = item

        def local_forward(stream_in, *params):
            return forward(stream_in, *params, length)
        result, pull = jax.vjp(local_forward, stream, *weights)
        grads = pull(grad_seq)
        live = (jnp.arange(SLOTS) < length)[:, None]
        grad_stream = jnp.where(live, grads[0], 0.0)
        carry = jax.tree.map(lambda total, piece: total + piece, carry, tuple(grads[1:]))
        return (carry, (result.astype(jnp.bfloat16), grad_stream))
    totals, (outputs, grad_streams) = lax.scan(one_sequence, totals, (streams, grads_in, owned))
    return (outputs.reshape(N_DP * SLOTS, D), grad_streams.reshape(N_DP * SLOTS, D), totals[0], totals[1], totals[2], totals[3], totals[4], totals[5])
```

```python
import functools

import jax
import jax.numpy as jnp
from jax import lax
from jax.experimental import pallas as pl
from jax.experimental.pallas import tpu as pltpu
from jax.sharding import PartitionSpec as P

HEAD_DIM = 64
AUG = 80
epsilon = 1e-05
rope_base = 160000.0
LOG2E = 1.4426950408889634

NN = (((1,), (0,)), ((), ()))
NT = (((1,), (1,)), ((), ()))
TN = (((0,), (0,)), ((), ()))


def dot(a, b, dims=NN):
    return lax.dot_general(a, b, dims, preferred_element_type=jnp.float32)


def cost(flops, size):
    return pl.CostEstimate(flops=flops, transcendentals=0, bytes_accessed=size)


def params(*sem):
    return pltpu.CompilerParams(dimension_semantics=sem, vmem_limit_bytes=60 * 2**20)


def layer_norm(stream, gain_vec):
    center = stream - jnp.mean(stream, axis=-1, keepdims=True)
    spread = jnp.mean(center * center, axis=-1, keepdims=True)
    return center * lax.rsqrt(spread + epsilon) * gain_vec


def rope_tables(length_all):
    index = jnp.arange(HEAD_DIM // 2).astype(jnp.float32)
    inverse = rope_base ** (-2.0 * index / HEAD_DIM)
    places = jnp.arange(length_all).astype(jnp.float32)
    angle = inverse[:, None] * places[None, :]
    return (jnp.cos(angle), jnp.sin(angle))


def geglu_mix(gate_part, up_part):
    return jax.nn.gelu(gate_part, approximate=False) * up_part


def project_kernel(halves, *refs):
    row_refs, (w_ref, cos_ref, sin_ref, q_ref, k_ref, v_ref, wt_ref) = refs[:halves], refs[halves:]
    width = q_ref.shape[0]
    heads = width // HEAD_DIM
    step = pl.program_id(0)

    @pl.when(step == 0)
    def _():
        wt_ref[...] = w_ref[...].T

    rows = row_refs[0][...]
    if halves == 2:
        rows = jnp.where(step < pl.num_programs(0) // 2, rows, row_refs[1][...])
    cosine, sine = cos_ref[...], sin_ref[...]
    half = HEAD_DIM // 2

    def turned(part, factor):
        raw = dot(wt_ref[part * width : (part + 1) * width, :], rows, NT)
        raw = raw.reshape(heads, 2, half, raw.shape[1])
        first, second = raw[:, 0], raw[:, 1]
        out = jnp.stack(
            [first * cosine - second * sine, second * cosine + first * sine], axis=1
        )
        return (out * factor).reshape(width, -1).astype(jnp.bfloat16)

    q_ref[...] = turned(0, HEAD_DIM**-0.5)
    k_ref[...] = turned(1, 1.0)
    v_ref[...] = dot(wt_ref[2 * width :, :], rows, NT).astype(jnp.bfloat16)


def half_specs(count, block, width, halves):
    if halves == 1:
        return [pl.BlockSpec((block, width), lambda i: (i, 0))]
    per = count // 2
    return [
        pl.BlockSpec((block, width), lambda i: (jnp.minimum(i, per - 1), 0)),
        pl.BlockSpec((block, width), lambda i: (jnp.maximum(i - per, 0), 0)),
    ]


def project(row_list, weight, cosine, sine):
    slots = sum(r.shape[0] for r in row_list)
    width = row_list[0].shape[1]
    local = weight.shape[1] // 3
    block = min(256, slots)
    count = slots // block
    out = jax.ShapeDtypeStruct((local, slots), jnp.bfloat16)
    spec = pl.BlockSpec((local, block), lambda i: (0, i))
    table = pl.BlockSpec((HEAD_DIM // 2, block), lambda i: (0, i))
    return pl.pallas_call(
        functools.partial(project_kernel, len(row_list)),
        grid=(count,),
        in_specs=half_specs(count, block, width, len(row_list))
        + [pl.BlockSpec((width, 3 * local), lambda i: (0, 0)), table, table],
        out_specs=[spec] * 3,
        out_shape=[out] * 3,
        scratch_shapes=[pltpu.VMEM((3 * local, width), jnp.bfloat16)],
        compiler_params=params("arbitrary"),
        cost_estimate=cost(6 * slots * width * local, 0),
        name="project",
    )(*row_list, weight, cosine, sine)


def aug_rows(ref, first, second=None):
    row = lax.broadcasted_iota(jnp.int32, (AUG - HEAD_DIM, ref.shape[1]), 0)
    out = jnp.where(row == 0, first, 0.0)
    if second is not None:
        out = jnp.where(row == 1, second, out)
    ref[HEAD_DIM:, :] = out.astype(jnp.bfloat16)


def forward_kernel(len_ref, q_ref, k_ref, v_ref, o_ref, l_ref, p_ref, qa, ka, va, kn, s_ref):
    slots = q_ref.shape[1]
    chunk = min(256, slots)
    chunks = slots // chunk

    @pl.when(pl.program_id(0) == 0)
    def _():
        place = lax.broadcasted_iota(jnp.int32, (1, slots), 1) + len_ref[1]
        place = jnp.where(place >= slots, place - slots, place)
        aug_rows(ka, jnp.where(place < len_ref[0], 0.0, -1e30))
        aug_rows(qa, 1.0)
        aug_rows(va, 1.0)

    qa[:HEAD_DIM, :] = q_ref[...]
    ka[:HEAD_DIM, :] = k_ref[...]
    va[:HEAD_DIM, :] = v_ref[...]
    kn[...] = ka[...].T

    def scores(index, slot):
        block = qa[:, pl.ds(pl.multiple_of(index * chunk, chunk), chunk)]
        top = None
        for c in range(chunks):
            part = dot(kn[c * chunk : (c + 1) * chunk, :], block)
            s_ref[slot, c * chunk : (c + 1) * chunk, :] = part
            part = jnp.max(part.reshape(chunk // 8, 8, chunk), axis=0)
            top = part if top is None else jnp.maximum(top, part)
        return jnp.max(top, axis=0, keepdims=True) * LOG2E

    def soft(index, slot, top):
        where = pl.ds(pl.multiple_of(index * chunk, chunk), chunk)
        total = jnp.zeros((AUG, chunk), jnp.float32)
        for c in range(chunks):
            part = jnp.exp2(s_ref[slot, c * chunk : (c + 1) * chunk, :] * LOG2E - top)
            part = part.astype(jnp.bfloat16)
            p_ref[0, c * chunk : (c + 1) * chunk, where] = part
            total = total + dot(va[:, c * chunk : (c + 1) * chunk], part)
        norm = total[HEAD_DIM : HEAD_DIM + 1, :]
        l_ref[0, :, where] = norm
        o_ref[:, where] = (total[:HEAD_DIM] / norm).astype(jnp.bfloat16)

    if chunks == 1:
        soft(0, 0, scores(0, 0))
        return

    def pair(index, top):
        one = scores(2 * index + 1, 1)
        soft(2 * index, 0, top)
        two = scores(jnp.minimum(2 * index + 2, chunks - 1), 0)
        soft(2 * index + 1, 1, one)
        return two

    lax.fori_loop(0, chunks // 2, pair, scores(0, 0))


def attend(bounds, queries, keys, values):
    local, slots = queries.shape
    heads = local // HEAD_DIM
    chunk = min(256, slots)
    spec = pl.BlockSpec((HEAD_DIM, slots), lambda h: (h, 0))
    return pl.pallas_call(
        forward_kernel,
        grid=(heads,),
        in_specs=[pl.BlockSpec(memory_space=pltpu.SMEM)] + [spec] * 3,
        out_specs=[
            spec,
            pl.BlockSpec((1, 1, slots), lambda h: (h, 0, 0)),
            pl.BlockSpec((1, slots, slots), lambda h: (h, 0, 0)),
        ],
        out_shape=[
            jax.ShapeDtypeStruct((local, slots), jnp.bfloat16),
            jax.ShapeDtypeStruct((heads, 1, slots), jnp.float32),
            jax.ShapeDtypeStruct((heads, slots, slots), jnp.bfloat16),
        ],
        scratch_shapes=[pltpu.VMEM((AUG, slots), jnp.bfloat16)] * 3
        + [
            pltpu.VMEM((slots, AUG), jnp.bfloat16),
            pltpu.VMEM((2, slots, chunk), jnp.float32),
        ],
        compiler_params=params("arbitrary"),
        cost_estimate=cost(1024 * slots * slots * heads, 2 * heads * slots * slots),
        name="attend",
    )(bounds, queries, keys, values)


def unturn(raw, cosine, sine):
    half = HEAD_DIM // 2
    first, second = raw[:half], raw[half:]
    return jnp.concatenate(
        [first * cosine + second * sine, second * cosine - first * sine], axis=0
    ).astype(jnp.bfloat16)


def backward_kernel(
    p_ref, q_ref, k_ref, v_ref, do_ref, o_ref, l_ref, cos_ref, sin_ref,
    dq_ref, dk_ref, dv_ref, doa, va, vn, don, qn, ds_ref, acc,
):
    slots = q_ref.shape[1]
    chunk = p_ref.shape[1]
    index = pl.program_id(1)

    @pl.when((pl.program_id(0) == 0) & (index == 0))
    def _():
        aug_rows(va, 1.0, 1.0)

    @pl.when(index == 0)
    def _():
        inverse = 1.0 / l_ref[0]
        grad = do_ref[...].astype(jnp.float32)
        delta = jnp.sum(grad * o_ref[...].astype(jnp.float32), axis=0, keepdims=True) * -inverse
        high = delta.astype(jnp.bfloat16).astype(jnp.float32)
        aug_rows(doa, high, delta - high)
        grad = (grad * inverse).astype(jnp.bfloat16)
        doa[:HEAD_DIM, :] = grad
        don[...] = grad.T
        qn[...] = q_ref[...].T
        va[:HEAD_DIM, :] = v_ref[...]
        vn[...] = va[...].T
        acc[...] = jnp.zeros_like(acc)

    where = pl.ds(pl.multiple_of(index * chunk, chunk), chunk)
    v_rows = vn[where, :]
    for c in range(slots // chunk):
        cols = slice(c * chunk, (c + 1) * chunk)
        part = dot(v_rows, doa[:, cols]).astype(jnp.bfloat16)
        ds_ref[:, cols] = part * p_ref[0, :, cols]
    dv = dot(p_ref[0], don[...])
    dk = dot(ds_ref[...], qn[...])
    dv_ref[...] = dv.T.astype(jnp.bfloat16)
    dk_ref[...] = unturn(dk.T, cos_ref[:, where], sin_ref[:, where])
    k_cols = k_ref[:, where]
    for c in range(slots // chunk):
        cols = slice(c * chunk, (c + 1) * chunk)
        acc[:, cols] += dot(k_cols, ds_ref[:, cols])

    @pl.when(index == pl.num_programs(1) - 1)
    def _():
        dq_ref[...] = unturn(acc[...] * HEAD_DIM**-0.5, cos_ref[...], sin_ref[...])


def attend_back(probs, queries, keys, values, grad, outs, norm, cosine, sine):
    local, slots = queries.shape
    heads = local // HEAD_DIM
    chunk = min(256, slots)
    spec = pl.BlockSpec((HEAD_DIM, slots), lambda h, i: (h, 0))
    part = pl.BlockSpec((HEAD_DIM, chunk), lambda h, i: (h, i))
    table = pl.BlockSpec((HEAD_DIM // 2, slots), lambda h, i: (0, 0))
    return pl.pallas_call(
        backward_kernel,
        grid=(heads, slots // chunk),
        in_specs=[
            pl.BlockSpec((1, chunk, slots), lambda h, i: (h, i, 0)),
            spec, spec, spec, spec, spec,
            pl.BlockSpec((1, 1, slots), lambda h, i: (h, 0, 0)),
            table, table,
        ],
        out_specs=[spec, part, part],
        out_shape=[jax.ShapeDtypeStruct((local, slots), jnp.bfloat16)] * 3,
        scratch_shapes=[
            pltpu.VMEM((AUG, slots), jnp.bfloat16),
            pltpu.VMEM((AUG, slots), jnp.bfloat16),
            pltpu.VMEM((slots, AUG), jnp.bfloat16),
            pltpu.VMEM((slots, HEAD_DIM), jnp.bfloat16),
            pltpu.VMEM((slots, HEAD_DIM), jnp.bfloat16),
            pltpu.VMEM((chunk, slots), jnp.bfloat16),
            pltpu.VMEM((HEAD_DIM, slots), jnp.float32),
        ],
        compiler_params=params("arbitrary", "arbitrary"),
        cost_estimate=cost(1664 * slots * slots * heads, 2 * heads * slots * slots),
        name="attend_back",
    )(probs, queries, keys, values, grad, outs, norm, cosine, sine)


def generic_device(tokens, cotangent, qkv_w, out_w, ffin_w, ffout_w, norm1, norm2, lengths, assign):
    local_rows = tokens.shape[0]
    width = tokens.shape[1]
    parts = lax.axis_size("tensor")
    slots = local_rows * parts
    group = lax.axis_index("dp")
    ranks = lax.axis_index("tensor")
    seq_ids = jnp.arange(assign.shape[0])
    owned = jnp.sum(jnp.where(seq_ids == group, assign, 0))
    length = jnp.sum(jnp.where(seq_ids == owned, lengths, 0))
    row_live = (ranks * local_rows + jnp.arange(local_rows) < length)[:, None]
    gathered = (
        lax.all_gather(qkv_w.astype(jnp.bfloat16), "dp", axis=0, tiled=True),
        lax.all_gather(out_w.astype(jnp.bfloat16), "dp", axis=1, tiled=True),
        lax.all_gather(ffin_w.astype(jnp.bfloat16), "dp", axis=0, tiled=True),
        lax.all_gather(ffout_w.astype(jnp.bfloat16), "dp", axis=1, tiled=True),
        lax.all_gather(norm1.astype(jnp.bfloat16), "dp", axis=0, tiled=True),
        lax.all_gather(norm2.astype(jnp.bfloat16), "dp", axis=0, tiled=True),
    )
    w_qkv, w_out, w_fin, w_fout, gain_low1, gain_low2 = gathered
    gain_one = gain_low1.astype(jnp.float32)
    gain_two = gain_low2.astype(jnp.float32)
    local_width = w_qkv.shape[2]
    hidden_here = w_fin.shape[2]
    w_qkv_flat = w_qkv.reshape(width, 3 * local_width)
    stream = tokens.astype(jnp.float32)
    normed_one = layer_norm(stream, gain_one).astype(jnp.bfloat16)
    full_one = lax.all_gather(normed_one, "tensor", axis=0, tiled=True)
    cosine, sine = rope_tables(slots)
    queries, keys_all, values_all = project([full_one], w_qkv_flat, cosine, sine)
    attended, norm, probs = attend(jnp.stack([length, jnp.int32(0)]), queries, keys_all, values_all)
    middle = stream + lax.psum_scatter(
        jnp.einsum("ot,od->td", attended, w_out, preferred_element_type=jnp.float32),
        "tensor",
        scatter_dimension=0,
        tiled=True,
    )
    normed_two = layer_norm(middle, gain_two).astype(jnp.bfloat16)
    in_mat = w_fin.reshape(width, 2 * hidden_here)
    ffn_rows = lax.all_gather(normed_two, "tensor", axis=0, tiled=True)
    gate_up = jnp.dot(ffn_rows, in_mat, preferred_element_type=jnp.float32).reshape(
        -1, 2, hidden_here
    )
    gate_part = gate_up[:, 0]
    up_part = gate_up[:, 1]
    hidden = geglu_mix(gate_part, up_part).astype(jnp.bfloat16)
    feed = lax.psum_scatter(
        jnp.dot(hidden, w_fout, preferred_element_type=jnp.float32).astype(jnp.bfloat16),
        "tensor",
        scatter_dimension=0,
        tiled=True,
    ).astype(jnp.float32)
    mixed = jnp.where(row_live, middle + feed, 0.0).astype(jnp.bfloat16)
    grad_out_rows = jnp.where(row_live, cotangent.astype(jnp.float32), 0.0)
    grad_low = grad_out_rows.astype(jnp.bfloat16)
    grad_rows_all = lax.all_gather(grad_low, "tensor", axis=0, tiled=True)
    grad_fout = jnp.einsum("rf,rd->fd", hidden, grad_rows_all, preferred_element_type=jnp.float32)
    grad_hidden = jnp.einsum("rd,fd->rf", grad_rows_all, w_fout, preferred_element_type=jnp.float32)
    _, geglu_pull = jax.vjp(geglu_mix, gate_part, up_part)
    grad_gate, grad_up = geglu_pull(grad_hidden)
    grad_proj = (
        jnp.stack([grad_gate, grad_up], axis=1).astype(jnp.bfloat16).reshape(-1, 2 * hidden_here)
    )
    grad_fin = jnp.einsum(
        "rd,rc->dc", ffn_rows, grad_proj, preferred_element_type=jnp.float32
    ).reshape(width, 2, hidden_here)
    grad_norm_two = lax.psum_scatter(
        jnp.einsum("rc,dc->rd", grad_proj, in_mat, preferred_element_type=jnp.float32),
        "tensor",
        scatter_dimension=0,
        tiled=True,
    )
    _, norm_two_pull = jax.vjp(layer_norm, middle, gain_two)
    grad_middle_norm, grad_gain_two = norm_two_pull(grad_norm_two)
    grad_middle = grad_out_rows + grad_middle_norm
    branch_low = grad_middle.astype(jnp.bfloat16)
    branch_full = lax.all_gather(branch_low, "tensor", axis=0, tiled=True)
    grad_wout = jnp.einsum("or,rd->od", attended, branch_full, preferred_element_type=jnp.float32)
    grad_attended = jnp.einsum("rd,od->or", branch_full, w_out, preferred_element_type=jnp.float32)
    grad_attended = grad_attended.astype(jnp.bfloat16)
    grads = attend_back(
        probs, queries, keys_all, values_all, grad_attended, attended, norm, cosine, sine
    )
    grad_project = jnp.concatenate(grads, axis=0)
    grad_wqkv = jnp.einsum(
        "rd,cr->dc", full_one, grad_project, preferred_element_type=jnp.float32
    ).reshape(width, 3, local_width)
    grad_norm_one = lax.psum_scatter(
        jnp.einsum("cr,dc->rd", grad_project, w_qkv_flat, preferred_element_type=jnp.float32).astype(
            jnp.bfloat16
        ),
        "tensor",
        scatter_dimension=0,
        tiled=True,
    ).astype(jnp.float32)
    _, norm_one_pull = jax.vjp(layer_norm, stream, gain_one)
    grad_stream_norm, grad_gain_one = norm_one_pull(grad_norm_one)
    grad_tokens = jnp.where(row_live, grad_middle + grad_stream_norm, 0.0)
    gain_one_sum, gain_two_sum = lax.psum((grad_gain_one, grad_gain_two), "tensor")
    summed = tuple(
        lax.psum_scatter(
            value.astype(jnp.bfloat16), "dp", scatter_dimension=axis, tiled=True
        ).astype(jnp.float32)
        for value, axis in (
            (grad_wqkv, 0),
            (grad_wout, 1),
            (grad_fin, 0),
            (grad_fout, 1),
            (gain_one_sum, 0),
            (gain_two_sum, 0),
        )
    )
    return (mixed, grad_tokens) + summed


def place_z(pieces, first, z):
    rows, columns = pieces[0].shape
    other = columns - first

    def kernel(s_ref, *refs):
        step = pl.program_id(0)
        for k in range(4):

            @pl.when(step == k)
            def _(k=k):
                refs[4][0] = refs[k][:, :first]
                refs[5][0] = refs[k][:, first:]

    full = pl.BlockSpec((rows, columns), lambda k, s: (0, 0))
    where = lambda k, s: (lax.rem(s[0] + (4 - k), 4), 0, 0)
    return pl.pallas_call(
        kernel,
        grid_spec=pltpu.PrefetchScalarGridSpec(
            num_scalar_prefetch=1,
            grid=(4,),
            in_specs=[full] * 4,
            out_specs=[pl.BlockSpec((1, rows, first), where), pl.BlockSpec((1, rows, other), where)],
        ),
        out_shape=[
            jax.ShapeDtypeStruct((4, rows, first), pieces[0].dtype),
            jax.ShapeDtypeStruct((4, rows, other), pieces[0].dtype),
        ],
        compiler_params=params("arbitrary"),
        cost_estimate=cost(0, 16 * rows * columns),
        name="place_z",
    )(z.reshape(1), *pieces)


def place(own, received, mine, name):
    count, rows, columns = own.shape

    def kernel(s_ref, own_ref, received_ref, out_ref):
        @pl.when(pl.program_id(0) == 0)
        def _():
            out_ref[0, 0] = own_ref[0]

        @pl.when(pl.program_id(0) == 1)
        def _():
            out_ref[0, 0] = received_ref[0]

    block = (1, rows, columns)
    return pl.pallas_call(
        kernel,
        grid_spec=pltpu.PrefetchScalarGridSpec(
            num_scalar_prefetch=1,
            grid=(2, count),
            in_specs=[
                pl.BlockSpec(block, lambda p, i, s: (jnp.where(p == 0, i, count - 1), 0, 0)),
                pl.BlockSpec(block, lambda p, i, s: (jnp.where(p == 0, 0, i), 0, 0)),
            ],
            out_specs=pl.BlockSpec(
                (1,) + block, lambda p, i, s: (i, jnp.where(p == 0, s[0], 1 - s[0]), 0, 0)
            ),
        ),
        out_shape=jax.ShapeDtypeStruct((count, 2, rows, columns), own.dtype),
        compiler_params=params("arbitrary", "arbitrary"),
        cost_estimate=cost(0, 8 * own.size),
        name=name,
    )(mine.reshape(1), own, received)


def dp_perm(kind, amount=1):
    def target(i):
        z, y, x = i // 4, (i // 2) % 2, i % 2
        if kind == "x":
            x = 1 - x
        elif kind == "y":
            y = 1 - y
        else:
            z = (z + amount) % 4
        return z * 4 + y * 2 + x

    return [(i, target(i)) for i in range(16)]


def swap(value):
    return lax.ppermute(value, "tensor", [(0, 1), (1, 0)])


def send(value, kind, amount=1):
    return lax.ppermute(value, "dp", dp_perm(kind, amount))


def coords():
    group = lax.axis_index("dp")
    return group // 4, (group // 2) % 2, group % 2


def gather_group(local, first):
    rows, columns = local.shape
    other = columns - first
    z, y, x = [c.astype(jnp.int32) for c in coords()]
    pieces = [local] + [send(local, "z", k) for k in (1, 2, 3)]
    a0, b0 = place_z(pieces, first, z)
    ra, rb = send(a0, "x"), send(b0, "y")
    a1 = place(a0, ra, x, "place_x").reshape(4, 2 * rows, first)
    b1 = place(b0, rb, y, "place_y").reshape(8, rows, other)
    ra, rb = send(a1, "y"), send(b1, "x")
    a2 = place(a1, ra, y, "place_y")
    b2 = place(b1, rb, x, "place_x")
    return a2.reshape(16 * rows, first), b2.reshape(16 * rows, other)


def pick(value, index, axis):
    return lax.dynamic_index_in_dim(value, index, axis, keepdims=False)


def add(*values):
    return sum(v.astype(jnp.float32) for v in values)


def scatter_group(ga, gb):
    z, y, x = coords()
    rows = ga.shape[0] // 16
    ga = ga.reshape(4, 2, 2, rows, -1)
    gb = gb.reshape(4, 2, 2, rows, -1)
    low = jnp.bfloat16
    ra, rb = send(pick(ga, 1 - y, 1), "y"), send(pick(gb, 1 - x, 2), "x")
    a1 = add(pick(ga, y, 1), ra).astype(low)
    b1 = add(pick(gb, x, 2), rb).astype(low)
    ra, rb = send(pick(a1, 1 - x, 1), "x"), send(pick(b1, 1 - y, 1), "y")
    a2 = add(pick(a1, x, 1), ra).astype(low)
    b2 = add(pick(b1, y, 1), rb).astype(low)
    both = jnp.concatenate([a2, b2], axis=2)
    parts = [send(pick(both, (z + k) % 4, 0), "z", k) for k in (1, 2, 3)]
    return add(pick(both, z, 0), *parts)


def out_kernel(o_ref, w_ref, y_ref):
    y_ref[...] = dot(o_ref[...].T, w_ref[...], NT).astype(y_ref.dtype)


def out_other(outs, weight, rows):
    local = outs.shape[0]
    width = weight.shape[0]
    block = 256
    skip = rows // block
    return pl.pallas_call(
        out_kernel,
        grid=(rows // block,),
        in_specs=[
            pl.BlockSpec((local, block), lambda i: (0, i + skip)),
            pl.BlockSpec((width, local), lambda i: (0, 0)),
        ],
        out_specs=pl.BlockSpec((block, width), lambda i: (i, 0)),
        out_shape=jax.ShapeDtypeStruct((rows, width), jnp.bfloat16),
        compiler_params=params("arbitrary"),
        cost_estimate=cost(2 * rows * width * local, 0),
        name="out_other",
    )(outs, weight)


def normal(value):
    center = value - jnp.mean(value, axis=-1, keepdims=True)
    spread = lax.rsqrt(jnp.mean(center * center, axis=-1, keepdims=True) + epsilon)
    return center * spread, spread


def middle_kernel(o_ref, w_ref, x_ref, r_ref, h_ref, n_ref):
    value = dot(o_ref[...].T, w_ref[...], NT)
    value = value + (x_ref[...].astype(jnp.float32) + r_ref[...].astype(jnp.float32))
    h_ref[...] = value
    n_ref[...] = normal(value)[0].astype(jnp.bfloat16)


def middle_own(outs, weight, tokens, received):
    local = outs.shape[0]
    rows, width = tokens.shape
    block = 256
    spec = pl.BlockSpec((block, width), lambda i: (i, 0))
    return pl.pallas_call(
        middle_kernel,
        grid=(rows // block,),
        in_specs=[
            pl.BlockSpec((local, block), lambda i: (0, i)),
            pl.BlockSpec((width, local), lambda i: (0, 0)),
            spec,
            spec,
        ],
        out_specs=[spec, spec],
        out_shape=[
            jax.ShapeDtypeStruct((rows, width), jnp.float32),
            jax.ShapeDtypeStruct((rows, width), jnp.bfloat16),
        ],
        compiler_params=params("arbitrary"),
        cost_estimate=cost(2 * rows * width * local, 0),
        name="middle_own",
    )(outs, weight, tokens, received)


def geglu(gate, up, grad):
    size = jnp.abs(gate) * 0.7071067811865476
    bell = jnp.exp(-(size * size))
    t = 1.0 / (1.0 + 0.3275911 * size)
    poly = t * (
        0.254829592
        + t * (-0.284496736 + t * (1.421413741 + t * (-1.453152027 + t * 1.061405429)))
    )
    below = 0.5 * poly * bell
    phi = jnp.where(gate >= 0, 1.0 - below, below)
    act = gate * phi
    slope = phi + gate * bell * 0.3989422804014327
    return act * up, grad * up * slope, grad * act


def ffn_kernel(
    n_ref, y_ref, g_ref, u_ref, d_ref, t_ref,
    feed_ref, e_ref, hid_ref, dg_ref, du_ref, et_ref, ft_ref, facc, eacc,
):
    step = pl.program_id(0)
    rows = n_ref.shape[0]
    part = min(512, rows)
    low = jnp.bfloat16
    for start in range(0, rows, part):
        where = slice(start, start + part)
        gate = dot(n_ref[where, :], g_ref[...])
        up = dot(n_ref[where, :], u_ref[...])
        grad = dot(y_ref[where, :], d_ref[...])
        hid, dg, du = geglu(gate, up, grad)
        hid_ref[where, :] = hid.astype(low)
        dg_ref[where, :] = dg.astype(low)
        du_ref[where, :] = du.astype(low)

    @pl.when(step == 0)
    def _():
        facc[...] = dot(hid_ref[...], d_ref[...], NT)
        eacc[...] = dot(dg_ref[...], g_ref[...], NT) + dot(du_ref[...], u_ref[...], NT)

    @pl.when(step > 0)
    def _():
        facc[...] += dot(hid_ref[...], d_ref[...], NT)
        eacc[...] += dot(dg_ref[...], g_ref[...], NT) + dot(du_ref[...], u_ref[...], NT)

    @pl.when(step == pl.num_programs(0) - 1)
    def _():
        first = dot(n_ref[...], t_ref[...])
        grad = dot(y_ref[...], t_ref[...])
        lane = lax.broadcasted_iota(jnp.int32, first.shape, 1)
        up = pltpu.roll(first, 96, 1)
        grad = pltpu.roll(grad, 64, 1)
        live = lane < 32
        hid, dg, du = geglu(first, up, grad)
        hid = jnp.where(live, hid, 0.0)
        dg = jnp.where(live, dg, 0.0)
        du = jnp.where(live, du, 0.0)
        et = (dg + pltpu.roll(du, 32, 1)).astype(low)
        ft = pltpu.roll(hid, 64, 1).astype(low)
        et_ref[...] = et
        ft_ref[...] = ft
        feed_ref[...] = (facc[...] + dot(ft, t_ref[...], NT)).astype(low)
        e_ref[...] = (eacc[...] + dot(et, t_ref[...], NT)).astype(low)


def ffn(normed, grad_rows, w_in, w_down, w_tail):
    rows, width = normed.shape
    main = w_down.shape[1]
    block = 256
    count = main // block
    full = pl.BlockSpec((rows, width), lambda j: (0, 0))
    chunk = pl.BlockSpec((rows, block), lambda j: (0, j))
    last = pl.BlockSpec((rows, 128), lambda j: (0, 0))
    low = jnp.bfloat16
    return pl.pallas_call(
        ffn_kernel,
        grid=(count,),
        in_specs=[
            full,
            full,
            pl.BlockSpec((width, block), lambda j: (0, j)),
            pl.BlockSpec((width, block), lambda j: (0, j + count)),
            pl.BlockSpec((width, block), lambda j: (0, j)),
            pl.BlockSpec((width, 128), lambda j: (0, 0)),
        ],
        out_specs=[full, full, chunk, chunk, chunk, last, last],
        out_shape=[
            jax.ShapeDtypeStruct((rows, width), low),
            jax.ShapeDtypeStruct((rows, width), low),
        ]
        + [jax.ShapeDtypeStruct((rows, main), low)] * 3
        + [jax.ShapeDtypeStruct((rows, 128), low)] * 2,
        scratch_shapes=[pltpu.VMEM((rows, width), jnp.float32)] * 2,
        compiler_params=params("arbitrary"),
        cost_estimate=cost(12 * rows * width * main, 0),
        name="ffn",
    )(normed, grad_rows, w_in, w_in, w_down, w_tail)


def weight_grad(lefts, rights, flip, name):
    rows, width = lefts[0].shape
    pairs = len(lefts)
    kinds = len(rights[0])
    columns = [r.shape[0] if flip else r.shape[1] for r in rights[0]]
    block = 256
    dims = NT if flip else NN

    def kernel(*refs):
        left = refs[:pairs]
        right = refs[pairs : pairs + pairs * kinds]
        out = refs[-1]
        turned = [r[...].T for r in left]
        start = 0
        for kind in range(kinds):
            total = None
            for p in range(pairs):
                value = dot(turned[p], right[p * kinds + kind][...], dims)
                total = value if total is None else total + value
            out[:, start : start + columns[kind]] = total.astype(jnp.bfloat16)
            start += columns[kind]

    flat = [r for group in rights for r in group]

    def right_spec(index, value):
        if not flip:
            return pl.BlockSpec(value.shape, lambda i: (0, 0))
        half = index // kinds
        return pl.BlockSpec((value.shape[0], rows), lambda i: (0, half))

    return pl.pallas_call(
        kernel,
        grid=(width // block,),
        in_specs=[pl.BlockSpec((rows, block), lambda i: (0, i))] * pairs
        + [right_spec(i, v) for i, v in enumerate(flat)],
        out_specs=pl.BlockSpec((block, sum(columns)), lambda i: (i, 0)),
        out_shape=jax.ShapeDtypeStruct((width, sum(columns)), jnp.bfloat16),
        compiler_params=params("arbitrary"),
        cost_estimate=cost(2 * pairs * rows * width * sum(columns), 0),
        name=name,
    )(*lefts, *flat)


def tail_grad(normed, grad_rows, et, ft):
    rows, width = normed[0].shape
    block = 256

    def kernel(n0, n1, y0, y1, e0, e1, f0, f1, out):
        total = dot(n0[...].T, e0[...]) + dot(n1[...].T, e1[...])
        total = total + dot(y0[...].T, f0[...]) + dot(y1[...].T, f1[...])
        out[...] = total.astype(jnp.bfloat16)

    left = pl.BlockSpec((rows, block), lambda i: (0, i))
    right = pl.BlockSpec((rows, 128), lambda i: (0, 0))
    return pl.pallas_call(
        kernel,
        grid=(width // block,),
        in_specs=[left] * 4 + [right] * 4,
        out_specs=pl.BlockSpec((block, 128), lambda i: (i, 0)),
        out_shape=jax.ShapeDtypeStruct((width, 128), jnp.bfloat16),
        compiler_params=params("arbitrary"),
        cost_estimate=cost(8 * rows * width * 128, 0),
        name="tail_grad",
    )(*normed, *grad_rows, *et, *ft)


def norm_pull(value, grad):
    unit, spread = normal(value)
    return spread * (
        grad
        - jnp.mean(grad, axis=-1, keepdims=True)
        - unit * jnp.mean(grad * unit, axis=-1, keepdims=True)
    )


def two_kernel(len_ref, h_ref, e_ref, er_ref, f_ref, fr_ref, y_ref, dh_ref, low_ref, mixed_ref):
    block = h_ref.shape[0]
    value = h_ref[...]
    grad = e_ref[...].astype(jnp.float32) + er_ref[...].astype(jnp.float32)
    back = y_ref[...].astype(jnp.float32) + norm_pull(value, grad)
    dh_ref[...] = back
    low_ref[...] = back.astype(jnp.bfloat16)
    feed = f_ref[...].astype(jnp.float32) + fr_ref[...].astype(jnp.float32)
    place = lax.broadcasted_iota(jnp.int32, value.shape, 0) + pl.program_id(0) * block
    mixed_ref[...] = jnp.where(place < len_ref[0], value + feed, 0.0).astype(jnp.bfloat16)


def norm_two_back(live, middle, grad, grad_other, feed, feed_other, grad_rows):
    rows, width = middle.shape
    block = 256
    spec = pl.BlockSpec((block, width), lambda i: (i, 0))
    return pl.pallas_call(
        two_kernel,
        grid=(rows // block,),
        in_specs=[pl.BlockSpec(memory_space=pltpu.SMEM)] + [spec] * 6,
        out_specs=[spec] * 3,
        out_shape=[
            jax.ShapeDtypeStruct((rows, width), jnp.float32),
            jax.ShapeDtypeStruct((rows, width), jnp.bfloat16),
            jax.ShapeDtypeStruct((rows, width), jnp.bfloat16),
        ],
        compiler_params=params("arbitrary"),
        cost_estimate=cost(0, 20 * rows * width),
        name="norm_two_back",
    )(live, middle, grad, grad_other, feed, feed_other, grad_rows)


def one_kernel(len_ref, x_ref, e_ref, er_ref, dh_ref, out_ref):
    block = x_ref.shape[0]
    grad = e_ref[...].astype(jnp.float32) + er_ref[...].astype(jnp.float32)
    back = dh_ref[...] + norm_pull(x_ref[...].astype(jnp.float32), grad)
    place = lax.broadcasted_iota(jnp.int32, back.shape, 0) + pl.program_id(0) * block
    out_ref[...] = jnp.where(place < len_ref[0], back, 0.0)


def norm_one_back(live, tokens, grad, grad_other, grad_middle):
    rows, width = tokens.shape
    block = 256
    spec = pl.BlockSpec((block, width), lambda i: (i, 0))
    return pl.pallas_call(
        one_kernel,
        grid=(rows // block,),
        in_specs=[pl.BlockSpec(memory_space=pltpu.SMEM)] + [spec] * 4,
        out_specs=spec,
        out_shape=jax.ShapeDtypeStruct((rows, width), jnp.float32),
        compiler_params=params("arbitrary"),
        cost_estimate=cost(0, 14 * rows * width),
        name="norm_one_back",
    )(live, tokens, grad, grad_other, grad_middle)


def grad_out_kernel(own_ref, other_ref, w_ref, out_ref, wt_ref):
    step = pl.program_id(0)

    @pl.when(step == 0)
    def _():
        wt_ref[...] = w_ref[...].T

    rows = jnp.where(step < pl.num_programs(0) // 2, own_ref[...], other_ref[...])
    out_ref[...] = dot(wt_ref[...], rows, NT).astype(jnp.bfloat16)


def grad_outs(own, other, weight):
    rows, width = own.shape
    local = weight.shape[1]
    block = 256
    count = 2 * rows // block
    return pl.pallas_call(
        grad_out_kernel,
        grid=(count,),
        in_specs=half_specs(count, block, width, 2)
        + [pl.BlockSpec((width, local), lambda i: (0, 0))],
        out_specs=pl.BlockSpec((local, block), lambda i: (0, i)),
        out_shape=jax.ShapeDtypeStruct((local, 2 * rows), jnp.bfloat16),
        scratch_shapes=[pltpu.VMEM((local, width), jnp.bfloat16)],
        compiler_params=params("arbitrary"),
        cost_estimate=cost(4 * rows * width * local, 0),
        name="grad_outs",
    )(own, other, weight)


def input_grad(grads, weights, rows, half, name):
    width = weights[0].shape[0]
    block = 256
    skip = half * (rows // block)
    flat = [g for group in grads for g in group]
    kinds = len(grads[0])

    def kernel(*refs):
        out = refs[-1]
        total = None
        for index in range(len(weights)):
            cols = jnp.concatenate(
                [r[...] for r in refs[index * kinds : (index + 1) * kinds]], axis=0
            )
            value = dot(cols.T, refs[len(flat) + index][...], NT)
            total = value if total is None else total + value
        out[...] = total.astype(jnp.bfloat16)

    return pl.pallas_call(
        kernel,
        grid=(rows // block,),
        in_specs=[pl.BlockSpec((g.shape[0], block), lambda i: (0, i + skip)) for g in flat]
        + [pl.BlockSpec(w.shape, lambda i: (0, 0)) for w in weights],
        out_specs=pl.BlockSpec((block, width), lambda i: (i, 0)),
        out_shape=jax.ShapeDtypeStruct((rows, width), jnp.bfloat16),
        compiler_params=params("arbitrary"),
        cost_estimate=cost(2 * rows * sum(w.size for w in weights), 0),
        name=name,
    )(*flat, *weights)


def fast_device(tokens, cotangent, qkv_w, out_w, ffin_w, ffout_w, norm1, norm2, lengths, assign):
    low = jnp.bfloat16
    rows, width = tokens.shape
    slots = 2 * rows
    group = lax.axis_index("dp")
    rank = lax.axis_index("tensor")
    seq_ids = jnp.arange(assign.shape[0])
    owned = jnp.sum(jnp.where(seq_ids == group, assign, 0))
    length = jnp.sum(jnp.where(seq_ids == owned, lengths, 0)).astype(jnp.int32)
    offset = (rank * rows).astype(jnp.int32)
    live = length - offset
    bounds = jnp.stack([length, offset])
    live_one = live.reshape(1)

    shard = qkv_w.shape[0]
    local = qkv_w.shape[2]
    hidden = ffin_w.shape[2]
    main = hidden // 256 * 256
    rest = hidden - main
    gain1 = norm1.astype(low).astype(jnp.float32)[:, None]
    gain2 = norm2.astype(low).astype(jnp.float32)[:, None]
    qkv_low = qkv_w.astype(low).astype(jnp.float32)
    fin_low = ffin_w.astype(low).astype(jnp.float32)
    half = local // 2
    qkv_scaled = (qkv_low * gain1[:, :, None]).astype(low)
    fin_scaled = (fin_low * gain2[:, :, None]).astype(low)
    qkv_local = jnp.concatenate(
        [qkv_scaled[:, :, i * half : (i + 1) * half].reshape(shard, 3 * half) for i in (0, 1)],
        axis=1,
    )
    down = ffout_w.astype(low).T
    ffn_local = jnp.concatenate(
        [
            fin_scaled[:, 0, :main],
            fin_scaled[:, 1, :main],
            down[:, :main],
            fin_scaled[:, 0, main:],
            fin_scaled[:, 1, main:],
            down[:, main:],
            jnp.zeros((shard, 128 - 3 * rest), low),
            out_w.astype(low).T,
        ],
        axis=1,
    )
    stream = tokens.astype(jnp.float32)
    one_own = normal(stream)[0].astype(low)
    row_live = (jnp.arange(rows) < live)[:, None]
    dy_own = jnp.where(row_live, cotangent, jnp.zeros_like(cotangent))
    one_other = swap(one_own)
    dy_other = swap(dy_own)
    w_a, w_b = gather_group(qkv_local, 3 * half)
    w_in, w_rest = gather_group(ffn_local, 2 * main)
    w_down = w_rest[:, :main]
    w_tail = w_rest[:, main : main + 128]
    w_out = w_rest[:, main + 128 :]

    cosine, sine = rope_tables(slots)
    order = lambda t: jnp.where(rank == 0, t, jnp.roll(t, rows, axis=1))
    cosine, sine = order(cosine), order(sine)
    groups = []
    for weight in (w_a, w_b):
        q, k, v = project([one_own, one_other], weight, cosine, sine)
        o, norm, probs = attend(bounds, q, k, v)
        groups.append((q, k, v, o, norm, probs))
    outs = jnp.concatenate([g[3] for g in groups], axis=0)
    received = swap(out_other(outs, w_out, rows))
    middle, two_own = middle_own(outs, w_out, tokens, received)
    two_other = swap(two_own)
    feed_own, e_own, hid0, dg0, du0, et0, ft0 = ffn(two_own, dy_own, w_in, w_down, w_tail)
    feed_send, e_send, hid1, dg1, du1, et1, ft1 = ffn(two_other, dy_other, w_in, w_down, w_tail)
    e_other = swap(e_send)
    feed_other = swap(feed_send)
    g_down = weight_grad([dy_own, dy_other], [[hid0], [hid1]], False, "grad_down")
    back, back_own, mixed = norm_two_back(
        live_one, middle, e_own, e_other, feed_own, feed_other, dy_own
    )
    back_other = swap(back_own)
    g_in = weight_grad([two_own, two_other], [[dg0, du0], [dg1, du1]], False, "grad_in")
    g_tail = tail_grad((two_own, two_other), (dy_own, dy_other), (et0, et1), (ft0, ft1))
    grad_att = grad_outs(back_own, back_other, w_out)
    g_out = weight_grad([back_own, back_other], [[outs], [outs]], True, "grad_out")
    ffn_sum = scatter_group(g_in, jnp.concatenate([g_down, g_tail, g_out], axis=1))
    grads = []
    sums = []
    for index, (q, k, v, o, norm, probs) in enumerate(groups):
        piece = grad_att[index * half : (index + 1) * half]
        grads.append(attend_back(probs, q, k, v, piece, o, norm, cosine, sine))
        sums.append(
            weight_grad([one_own, one_other], [grads[-1], grads[-1]], True, f"grad_qkv{index}")
        )
    qkv_sum = scatter_group(*sums)
    e1_send = input_grad(grads, (w_a, w_b), rows, 1, "input_other")
    e1_other = swap(e1_send)
    e1_own = input_grad(grads, (w_a, w_b), rows, 0, "input_own")
    grad_tokens = norm_one_back(live_one, tokens, e1_own, e1_other, back)

    qkv_sum = qkv_sum.reshape(shard, 2, 3, half).transpose(0, 2, 1, 3).reshape(shard, 3, local)
    gate_sum = jnp.concatenate(
        [ffn_sum[:, :main], ffn_sum[:, 3 * main : 3 * main + rest]], axis=1
    )
    up_sum = jnp.concatenate(
        [ffn_sum[:, main : 2 * main], ffn_sum[:, 3 * main + rest : 3 * main + 2 * rest]], axis=1
    )
    down_sum = jnp.concatenate(
        [ffn_sum[:, 2 * main : 3 * main], ffn_sum[:, 3 * main + 2 * rest : 3 * main + 3 * rest]],
        axis=1,
    )
    fin_sum = jnp.stack([gate_sum, up_sum], axis=1)
    out_sum = ffn_sum[:, 3 * main + 128 :]
    gains = jnp.stack(
        [jnp.sum(qkv_sum * qkv_low, axis=(1, 2)), jnp.sum(fin_sum * fin_low, axis=(1, 2))]
    )
    gains = gains + swap(gains)
    return (
        mixed,
        grad_tokens,
        qkv_sum * gain1[:, :, None],
        out_sum.T,
        fin_sum * gain2[:, :, None],
        down_sum.T,
        gains[0],
        gains[1],
    )


def solution(mesh):
    specs = (
        P(("dp", "tensor"), None),
        P(("dp", "tensor"), None),
        P("dp", None, "tensor"),
        P("tensor", "dp"),
        P("dp", None, "tensor"),
        P("tensor", "dp"),
        P("dp"),
        P("dp"),
    )
    paired = mesh.shape["dp"] == 16 and mesh.shape["tensor"] == 2
    return jax.shard_map(
        fast_device if paired else generic_device,
        mesh=mesh,
        in_specs=specs + (P(), P()),
        out_specs=specs,
        check_vma=False,
    )
```
